32 devices in a mesh: groups: 2 (over x), pen: 16 (over z, y, core).
Axes of the slice: x: 2, y: 2, z: 4, core: 2. Of those that a mesh axis runs over, the one named last changes fastest.
Arguments:
- point_feat: bfloat16 [64, 65536], P(None, ('groups', 'pen')), parts along dimension 1, may hold values from -6 to 6
- pair_kernel: bfloat16 [2048, 128, 128], P(('groups', 'pen')), parts along dimension 0, may hold values from -0.5 to 0.5
- pair_owner: int32 [2048, 1], P(('groups', 'pen')), parts along dimension 0, may hold values from 0 to 15; in each aligned block of 64 rows (0 to 63, 64 to 127, ...) at most 8 rows name the same one
- pair_block: int32 [2048], P(('groups', 'pen')), parts along dimension 0, may hold values from 0 to 255
- spec_weight: bfloat16 [2, 256, 16, 64, 128], P(None, 'pen'), may hold values from -3 to 3
- mlp_up: bfloat16 [2, 256, 64], replicated, may hold values from -0.75 to 0.75
- mlp_down: bfloat16 [2, 64, 256], replicated, may hold values from -0.375 to 0.375
Outputs:
- point_out: float32 [64, 65536], P(None, ('groups', 'pen')), parts along dimension 1
The draws below stay inside these ranges and needn't reach their ends.
There are 2 independent parts, one for each index of `groups`. The reference program is written for one: setup_inputs(seed, part) draws one part's arguments, and reference() takes and returns one part's arrays. A program takes and returns all parts, laid end to end along the dimension named above; an argument that names none is the same for every part. Nothing has to cross between parts.
Inputs may be any that keep to these rules, and one draw needn't show every extreme that they name: `pair_owner`: among the pairs of one device, no device is named more than 8 times.
All inputs are finite; a program needn't handle non-finite values.
Results may differ from the reference program's by a relative error of at most 0.0055.
Values may be sent and summed in bfloat16 or wider, within the bound.
A program may use at most 128 MiB of HBM per device.

```python
import math
import jax
import jax.numpy as jnp
import numpy as np
from jax import lax

C = 64
HID = 256
NX = 128
NY = 64
NZ = 64
MX = 16
MY = 16
MZ = 16
LAYERS = 2
BS = 128
NBR = 4
BLK_DEV = 16
CAP = 8
PAIRS = 1024
NPTS = 32768
GB_DEV = 256
N_PEN = 16


def set_ends(values, rng, least, top_value):
    extent = values.shape
    place = [jax.random.randint(jax.random.fold_in(rng, axis), (), 0, extent[axis]) for axis in range(len(extent))]
    values = values.at[tuple(place)].set(least)
    longest = extent.index(max(extent))
    place[longest] = (place[longest] + 1) % extent[longest]
    return values.at[tuple(place)].set(top_value)


def block_levels(stream_key, shape, pieces, low, top_value):
    def one(dim, shards_of):
        steps = jax.random.uniform(jax.random.fold_in(jax.random.fold_in(stream_key, 6), dim), (shards_of,), jnp.float32, low / len(pieces), top_value / len(pieces))
        return jnp.repeat(jnp.exp(steps), shape[dim] // shards_of).reshape((-1,) + (1,) * (len(shape) - dim - 1))

    factor_of = one(*pieces[0])
    for cut in pieces[1:]:
        factor_of = factor_of * one(*cut)
    return factor_of


def assign_block(stream_key, own, number, rows, amount, top, most, lean):
    ranking = jax.random.permutation(stream_key, amount)
    heavy_load, common = shares(amount, rows * top, most, lean, True), shares(amount, rows * top, most, lean, False)
    places = jnp.arange(amount)

    def named(lengths, turn):
        used = int((lengths > 0).sum())
        fixed = max(1, used // 4)
        passed = fixed + (places - fixed + turn * (used - fixed)) % max(1, amount - fixed)
        return jnp.zeros((amount,), jnp.int32).at[ranking[jnp.where(places < fixed, places, passed)]].set(jnp.asarray(lengths, jnp.int32))

    lengths = jnp.where(number % 4 == 0, named(heavy_load, number // 4), named(common, number - number // 4 - 1))
    mixed = jax.random.permutation(jax.random.fold_in(own, 3), amount)
    source_of, receiver = mixed[0:amount // 2 * 2:2], mixed[1:amount // 2 * 2:2]
    room = jnp.minimum(lengths[source_of] - 1, most - lengths[receiver]) // 2
    room = jnp.where((source_of == ranking[0]) | (receiver == ranking[0]) | (lengths[receiver] == 0), 0, jnp.maximum(room, 0))
    passed = jax.random.randint(jax.random.fold_in(own, 4), (amount // 2,), 0, 1 << 20) % (room + 1)
    lengths = lengths.at[source_of].add(-passed).at[receiver].add(passed)
    members = jnp.searchsorted(jnp.cumsum(lengths), jnp.arange(rows * top), side="right").astype(jnp.int32)
    table = members.reshape(top, rows).T
    table = table[jax.random.permutation(jax.random.fold_in(own, 1), rows)]
    turn = jax.random.randint(jax.random.fold_in(own, 2), (rows, 1), 0, top)
    return jnp.take_along_axis(table, (jnp.arange(top)[None, :] + turn) % top, axis=1)


def shares(number_of, total, limit, skew, full):
    portions = [(1 << 20) // math.isqrt(grade ** skew) + 1 for grade in range(1, number_of + 1)]
    largest = limit if full else min(limit, max(-(-total // number_of), total * portions[0] // sum(portions)))
    least = 1 if total - largest >= number_of - 1 else 0
    counts, spare = [largest] + [least] * (number_of - 1), total - largest - least * (number_of - 1)
    while spare > 0:
        movable = [i for i in range(1, number_of) if counts[i] < largest] or [i for i in range(1, number_of) if counts[i] < limit]
        mass, remaining = sum([portions[i] for i in movable]), spare
        for i in movable:
            addition = min(limit - counts[i], max(1, remaining * portions[i] // mass), spare)
            counts[i] = counts[i] + addition
            spare = spare - addition
    return np.array(counts)


def noise(key, dims, scale, most, shards=(), held_as=jnp.bfloat16):
    factor_of = block_levels(key, dims, shards, -0.22, 0.18) if shards else 1.0
    drawn = jax.random.normal(key, dims, jnp.float32) * scale * factor_of
    return jnp.minimum(jnp.maximum(drawn, -most), most).astype(held_as)


def setup_inputs(seed: int = 0, part: int = 0) -> dict:
    arg_keys = jax.random.split(jax.random.key(seed), 8)
    own_keys = jax.random.split(jax.random.fold_in(arg_keys[7], part), 8)
    point_feat = noise(own_keys[0], (C, NPTS), 1.0, 6.0, ((1, 16),))
    pair_kernel = noise(own_keys[1], (PAIRS, BS, BS), BS ** -0.5, 0.5, ((0, 16),))
    pair_owner_keys = jax.random.split(jax.random.fold_in(own_keys[2], 1), PAIRS // (BLK_DEV * NBR))
    pair_owner_turns = jax.random.permutation(jax.random.fold_in(own_keys[2], 3), PAIRS // (BLK_DEV * NBR))
    pair_owner = jax.vmap(lambda own, number: assign_block(jax.random.fold_in(own_keys[2], 2), own, number, BLK_DEV * NBR, N_PEN, 1, CAP, 2))(pair_owner_keys, pair_owner_turns).reshape((PAIRS, 1))
    pair_block = set_ends(jax.random.randint(own_keys[3], (PAIRS,), 0, GB_DEV), jax.random.fold_in(own_keys[3], 1), 0, GB_DEV - 1).astype(jnp.int32)
    spec_weight = noise(arg_keys[4], (LAYERS, MY * MZ, MX, C, 2 * C), (C // 16) ** -0.5, 3.0, ((1, 16),))
    mlp_up = noise(arg_keys[5], (LAYERS, HID, C), C ** -0.5, 0.75)
    mlp_down = noise(arg_keys[6], (LAYERS, C, HID), HID ** -0.5, 0.375)
    return dict(point_feat=point_feat, pair_kernel=pair_kernel, pair_owner=pair_owner, pair_block=pair_block, spec_weight=spec_weight, mlp_up=mlp_up, mlp_down=mlp_down)


HIGHEST = lax.Precision.HIGHEST


def yz_tables():
    mode_index = jnp.arange(MY * MZ, dtype=jnp.int32)
    wave_y = mode_index // MZ - MY // 2
    wave_z = mode_index % MZ
    cell_index = jnp.arange(NY * NZ, dtype=jnp.int32)
    row_y = cell_index // NZ
    row_z = cell_index % NZ
    phase_turns = jnp.mod(row_y[:, None] * wave_y[None, :], NY).astype(jnp.float32) / NY + jnp.mod(row_z[:, None] * wave_z[None, :], NZ).astype(jnp.float32) / NZ
    angle = 2.0 * math.pi * phase_turns
    forward_table = jnp.stack([jnp.cos(angle), -jnp.sin(angle)], axis=2).reshape(NY * NZ, 2 * MY * MZ)
    scaling = jnp.where(wave_z == 0, 1.0, 2.0).astype(jnp.float32) / (NX * NY * NZ)
    inverse_table = forward_table * jnp.repeat(scaling, 2)[None, :]
    return forward_table, inverse_table


def along_tables(positions):
    wave_number = jnp.arange(MX, dtype=jnp.int32) - MX // 2
    angle = 2.0 * math.pi * jnp.mod(wave_number[:, None] * positions[None, :], NX).astype(jnp.float32) / NX
    return jnp.cos(angle), jnp.sin(angle)


def spectral_part(grid_field, weights_now, forward_table, inverse_table):
    modes_all = MY * MZ
    planar = jnp.dot(grid_field.reshape(C * NX, NY * NZ), forward_table, precision=HIGHEST).reshape(C, NX, modes_all, 2)
    cosine_table, sine_table = along_tables(jnp.arange(NX, dtype=jnp.int32))
    part_real = planar[..., 0]
    part_imag = planar[..., 1]
    modes_real = jnp.einsum("jx,cxm->mjc", cosine_table, part_real, precision=HIGHEST) + jnp.einsum("jx,cxm->mjc", sine_table, part_imag, precision=HIGHEST)
    modes_imag = jnp.einsum("jx,cxm->mjc", cosine_table, part_imag, precision=HIGHEST) - jnp.einsum("jx,cxm->mjc", sine_table, part_real, precision=HIGHEST)
    weight_real = weights_now[..., :C].astype(jnp.float32)
    weight_imag = weights_now[..., C:].astype(jnp.float32)
    mixed_real = jnp.einsum("mjc,mjco->mjo", modes_real, weight_real, precision=HIGHEST) - jnp.einsum("mjc,mjco->mjo", modes_imag, weight_imag, precision=HIGHEST)
    mixed_imag = jnp.einsum("mjc,mjco->mjo", modes_real, weight_imag, precision=HIGHEST) + jnp.einsum("mjc,mjco->mjo", modes_imag, weight_real, precision=HIGHEST)
    back_real = jnp.einsum("jx,mjo->oxm", cosine_table, mixed_real, precision=HIGHEST) - jnp.einsum("jx,mjo->oxm", sine_table, mixed_imag, precision=HIGHEST)
    back_imag = jnp.einsum("jx,mjo->oxm", sine_table, mixed_real, precision=HIGHEST) + jnp.einsum("jx,mjo->oxm", cosine_table, mixed_imag, precision=HIGHEST)
    joined = jnp.stack([back_real, back_imag], axis=3).reshape(C * NX, 2 * modes_all)
    return jnp.dot(joined, inverse_table.T, precision=HIGHEST).reshape(C, NX, NY * NZ)


def channel_mlp(summed, weight_up, weight_down):
    def one_plane(values):
        rounded = values.astype(jnp.bfloat16)
        hidden = jnp.dot(weight_up, rounded, preferred_element_type=jnp.float32)
        active = jax.nn.gelu(hidden, approximate=True).astype(jnp.bfloat16)
        return values + jnp.dot(weight_down, active, preferred_element_type=jnp.float32)

    planes_first = jnp.moveaxis(summed, 1, 0)
    return jnp.moveaxis(lax.map(one_plane, planes_first), 0, 1)


def reference(point_feat, pair_kernel, pair_owner, pair_block, spec_weight, mlp_up, mlp_down):
    grid_total = NX * NY * NZ // BS
    target = pair_owner[:, 0] * GB_DEV + pair_block
    feature_blocks = point_feat.reshape(C, PAIRS // NBR, BS).transpose(1, 0, 2)
    pair_features = jnp.repeat(feature_blocks, NBR, axis=0)
    kernels_wide = pair_kernel.astype(jnp.float32)
    contrib = jnp.einsum("pci,pij->pcj", pair_features.astype(jnp.float32), kernels_wide)
    grid_blocks = jax.ops.segment_sum(contrib, target, num_segments=grid_total)
    grid_field = grid_blocks.transpose(1, 0, 2).reshape(C, NX, NY * NZ)
    forward_table, inverse_table = yz_tables()
    for number in range(LAYERS):
        spectral = spectral_part(grid_field, spec_weight[number], forward_table, inverse_table)
        summed = grid_field + spectral
        grid_field = channel_mlp(summed, mlp_up[number], mlp_down[number])
    grid_out = grid_field.astype(jnp.bfloat16).reshape(C, grid_total, BS).transpose(1, 0, 2)
    fetched = grid_out[target]
    back = jnp.einsum("pcj,pij->pci", fetched.astype(jnp.float32), kernels_wide)
    summed_back = back.reshape(PAIRS // NBR, NBR, C, BS).sum(axis=1)
    return summed_back.transpose(1, 0, 2).reshape(C, NPTS)
```

```python
import functools
import math

import jax
import jax.numpy as jnp
import numpy as np
from jax import lax
from jax.experimental import pallas as pl
from jax.experimental.pallas import tpu as pltpu
from jax.sharding import PartitionSpec as P

NX = 128
NY = 64
NZ = 64
MX = 16
MY = 16
MZ = 16
LAYERS = 2
NBR = 4

F32 = jnp.float32
BF16 = jnp.bfloat16
VMEM = pl.BlockSpec(memory_space=pltpu.VMEM)
SMEM = pl.BlockSpec(memory_space=pltpu.SMEM)
NT = (((1,), (1,)), ((), ()))


def plane_table(devices, lanes):
    here = MY * MZ // devices
    row = np.arange(2 * MY * MZ)
    mode = row // (2 * here) * here + row % here
    imag = (row % (2 * here)) // here
    wave_y = mode // MZ - MY // 2
    wave_z = mode % MZ
    cell = np.arange(lanes)
    turns = np.mod(np.outer(wave_y, cell // NZ), NY) / NY + np.mod(np.outer(wave_z, cell % NZ), NZ) / NZ
    first = 2 * np.pi * turns + np.where(imag, np.pi / 2, 0.0)[:, None]
    tiles = NY * NZ // lanes
    step = 2 * np.pi * np.mod(np.outer(np.arange(tiles) * (lanes // NZ), wave_y), NY) / NY
    parts = [np.cos(first), np.sin(first), np.cos(step), np.sin(step)]
    cos0, sin0, cos_k, sin_k = lax.optimization_barrier(tuple(jnp.asarray(a, F32) for a in parts))
    return (cos0[None] * cos_k[:, :, None] - sin0[None] * sin_k[:, :, None]).astype(BF16)


def along_tables(devices):
    planes = NX // devices
    waves = np.arange(MX) - MX // 2
    angle = 2 * np.pi * np.mod(np.outer(waves, np.arange(NX)), NX) / NX
    cos = np.cos(angle).reshape(MX, devices, planes)
    sin = np.sin(angle).reshape(MX, devices, planes)
    to_real = np.stack([cos, sin], axis=2)
    to_imag = np.stack([-sin, cos], axis=2)
    forward = np.concatenate([to_real, to_imag], axis=0).reshape(2 * MX, 2 * NX)
    return jnp.asarray(forward, BF16), jnp.asarray(forward.T, BF16)


def encode_kernel(devices, cap, owner, block, feat, kern, send, slot_of, targets, count):
    pairs = kern.shape[0]
    size = kern.shape[1]

    def clear(d, carry):
        count[d] = 0
        for i in range(cap):
            targets[d * cap + i] = -1
        send[d] = jnp.zeros(send.shape[1:], BF16)
        return carry

    lax.fori_loop(0, devices, clear, 0)

    def one(b, carry):
        values = feat[:, pl.ds(pl.multiple_of(b * size, size), size)]
        for k in range(NBR):
            p = b * NBR + k
            d = owner[p]
            n = count[d]
            count[d] = n + 1
            slot_of[p] = d * cap + n
            targets[d * cap + n] = block[p]
            send[d, n] = jnp.dot(values, kern[p], preferred_element_type=F32).astype(BF16)
        return carry

    lax.fori_loop(0, pairs // NBR, one, 0)
    lane = lax.broadcasted_iota(jnp.int32, (16, size), 1)

    def note(d, carry):
        row = jnp.zeros((16, size), F32)
        for i in range(cap):
            row = jnp.where(lane == i, targets[d * cap + i].astype(F32), row)
        send[d, cap, 0:16, :] = row.astype(BF16)
        return carry

    lax.fori_loop(0, devices, note, 0)


def table_tile(table, k, wide):
    return jnp.concatenate([table[k * wide + i] for i in range(wide)], axis=1)


def gather_sums_kernel(cap, per_plane, wide, targets, got, table, field, spec, total):
    channels, size = got.shape[2], got.shape[3]
    chunk = wide * size
    tiles = table.shape[0] // wide

    def clear(k, carry):
        field[:, pl.ds(pl.multiple_of(k * chunk, chunk), chunk)] = jnp.zeros((field.shape[0], chunk), F32)
        return carry

    lax.fori_loop(0, tiles, clear, 0)

    def add(d, carry):
        for i in range(cap):
            t = targets[d * cap + i]

            @pl.when(t >= 0)
            def _():
                rows = pl.ds(pl.multiple_of(t // per_plane * channels, channels), channels)
                cols = pl.ds(pl.multiple_of(t % per_plane * size, size), size)
                field[rows, cols] += got[d, i].astype(F32)

        return carry

    lax.fori_loop(0, got.shape[0], add, 0)
    total[...] = jnp.zeros_like(total)

    def transform(k, carry):
        values = field[:, pl.ds(pl.multiple_of(k * chunk, chunk), chunk)].astype(BF16)
        total[...] += lax.dot_general(table_tile(table, k, wide), values, NT, preferred_element_type=F32)
        return carry

    lax.fori_loop(0, tiles, transform, 0)
    spec[...] = total[...].astype(BF16)


def mix_kernel(group, channels, forward, inverse, data, weight, out):
    rows = forward.shape[0]
    fan = weight.shape[1] // (2 * channels)
    row_wave = lax.broadcasted_iota(jnp.int32, (rows, 2 * channels), 0) % MX
    half = lax.broadcasted_iota(jnp.int32, (rows, 2 * channels), 1) // channels
    for g in range(group):
        modes = jnp.dot(forward[...], data[g], preferred_element_type=F32)
        twice = jnp.concatenate([modes, modes], axis=1)
        spread = jnp.concatenate(
            [jnp.where(row_wave == 2 * k + half, twice, 0.0).astype(BF16) for k in range(fan)], axis=1
        )
        prod = jnp.dot(spread, weight[g], preferred_element_type=F32)
        real, imag = prod[:MX], prod[MX:]
        mixed = jnp.concatenate(
            [
                real[:, :channels] - imag[:, channels:],
                real[:, channels:] + imag[:, :channels],
            ],
            axis=0,
        ).astype(BF16)
        out[g] = jnp.dot(inverse[...], mixed, preferred_element_type=F32).astype(BF16)


def layer_kernel(last, planes, wide, modes, table, field, up, down, out, *rest):
    channels = field.shape[0] // planes
    tile = table_tile(table, 0, wide)
    summed = out if not last else rest[0]
    summed[...] = field[...] + jnp.dot(modes[...], tile, preferred_element_type=F32)
    scale = math.sqrt(2.0 / math.pi)

    def one(p, carry):
        rows = pl.ds(pl.multiple_of(p * channels, channels), channels)
        values = summed[rows, :]
        v = jnp.dot(up[...], values.astype(BF16), preferred_element_type=F32)
        inner = v * (scale + (scale * 0.044715) * (v * v))
        halved = 0.5 * v
        active = (halved + halved * jnp.tanh(inner)).astype(BF16)
        values = values + jnp.dot(down[...], active, preferred_element_type=F32)
        out[rows, :] = values.astype(out.dtype)
        return carry

    lax.fori_loop(0, planes, one, 0)
    if not last:
        spec, total = rest

        @pl.when(pl.program_id(0) == 0)
        def _():
            total[...] = jnp.zeros_like(total)

        total[...] += lax.dot_general(tile, out[...].astype(BF16), NT, preferred_element_type=F32)

        @pl.when(pl.program_id(0) == pl.num_programs(0) - 1)
        def _():
            spec[...] = total[...].astype(BF16)


def pick_kernel(cap, per_plane, targets, field, send):
    channels, size = send.shape[2], send.shape[3]

    def one(d, carry):
        for i in range(cap):
            t = jnp.maximum(targets[d * cap + i], 0)
            rows = pl.ds(pl.multiple_of(t // per_plane * channels, channels), channels)
            cols = pl.ds(pl.multiple_of(t % per_plane * size, size), size)
            send[d, i] = field[rows, cols]
        return carry

    lax.fori_loop(0, send.shape[0], one, 0)


def decode_kernel(slot_of, got, kern, out):
    size = kern.shape[1]

    def one(b, carry):
        acc = None
        for k in range(NBR):
            p = b * NBR + k
            term = lax.dot_general(got[slot_of[p]], kern[p], NT, preferred_element_type=F32)
            acc = term if acc is None else acc + term
        out[:, pl.ds(pl.multiple_of(b * size, size), size)] = acc
        return carry

    lax.fori_loop(0, kern.shape[0] // NBR, one, 0)


def swap(values):
    return lax.all_to_all(values, "pen", split_axis=0, concat_axis=0, tiled=True)


def per_device(point_feat, pair_kernel, pair_owner, pair_block, spec_weight, mlp_up, mlp_down):
    devices = lax.axis_size("pen")
    pairs, size = pair_kernel.shape[0], pair_kernel.shape[1]
    channels = point_feat.shape[0]
    cap = 2 * pairs // devices
    planes = NX // devices
    plane_cells = NY * NZ
    per_plane = plane_cells // size
    here = spec_weight.shape[1]
    modes_all = MY * MZ
    hidden = mlp_up.shape[1]
    lines = planes * channels
    wide = 4
    table = plane_table(devices, size)
    forward, inverse = along_tables(devices)

    send, slot_of, targets = pl.pallas_call(
        functools.partial(encode_kernel, devices, cap),
        out_shape=(
            jax.ShapeDtypeStruct((devices, cap + 1, channels, size), BF16),
            jax.ShapeDtypeStruct((pairs,), jnp.int32),
            jax.ShapeDtypeStruct((devices * cap,), jnp.int32),
        ),
        in_specs=[SMEM, SMEM, VMEM, VMEM],
        out_specs=(VMEM, SMEM, SMEM),
        scratch_shapes=[pltpu.SMEM((devices,), jnp.int32)],
        name="encode",
    )(pair_owner[:, 0], pair_block, point_feat, pair_kernel)
    got = swap(send)
    wanted = got[:, cap, 0, :cap].astype(jnp.int32).reshape(devices * cap)

    field, spec = pl.pallas_call(
        functools.partial(gather_sums_kernel, cap, per_plane, wide),
        out_shape=(
            jax.ShapeDtypeStruct((lines, plane_cells), F32),
            jax.ShapeDtypeStruct((2 * modes_all, lines), BF16),
        ),
        in_specs=[SMEM, VMEM, VMEM],
        out_specs=(VMEM, VMEM),
        scratch_shapes=[pltpu.VMEM((2 * modes_all, lines), F32)],
        name="place",
    )(wanted, got, table)

    group = math.gcd(here, 4)
    first_mode = lax.axis_index("pen") * here
    wave_z = (first_mode + jnp.arange(here, dtype=jnp.int32)) % MZ
    scaling = jnp.where(wave_z == 0, 1.0, 2.0).astype(F32) / (NX * NY * NZ)
    for number in range(LAYERS):
        last = number == LAYERS - 1
        across = swap(spec.reshape(devices, 2 * here, lines))
        data = across.reshape(devices, 2, here, planes, channels).transpose(2, 0, 1, 3, 4)
        mixed = pl.pallas_call(
            functools.partial(mix_kernel, group, channels),
            out_shape=jax.ShapeDtypeStruct((here, 2 * NX, channels), BF16),
            grid=(here // group,),
            in_specs=[
                pl.BlockSpec((2 * MX, 2 * NX), lambda g: (0, 0)),
                pl.BlockSpec((2 * NX, 2 * MX), lambda g: (0, 0)),
                pl.BlockSpec((group, 2 * NX, channels), lambda g: (g, 0, 0)),
                pl.BlockSpec((group, MX * channels, 2 * channels), lambda g: (g, 0, 0)),
            ],
            out_specs=pl.BlockSpec((group, 2 * NX, channels), lambda g: (g, 0, 0)),
            name="mix",
        )(
            forward,
            inverse,
            data.reshape(here, 2 * NX, channels),
            spec_weight[number].reshape(here, MX * channels, 2 * channels),
        )
        mixed = mixed.astype(F32) * scaling[:, None, None]
        back = mixed.astype(BF16).reshape(here, devices, 2, planes, channels).transpose(1, 2, 0, 3, 4)
        modes = swap(back.reshape(devices, 2 * here, lines)).reshape(2 * modes_all, lines).T

        chunk = wide * size
        spec_shape = (2 * modes_all, lines)
        field_spec = pl.BlockSpec((lines, chunk), lambda k: (0, k))
        results = pl.pallas_call(
            functools.partial(layer_kernel, last, planes, wide),
            out_shape=(jax.ShapeDtypeStruct((lines, plane_cells), BF16 if last else F32),)
            + (() if last else (jax.ShapeDtypeStruct(spec_shape, BF16),)),
            grid=(plane_cells // chunk,),
            in_specs=[
                pl.BlockSpec((lines, 2 * modes_all), lambda k: (0, 0)),
                pl.BlockSpec((wide, 2 * modes_all, size), lambda k: (k, 0, 0)),
                field_spec,
                pl.BlockSpec((hidden, channels), lambda k: (0, 0)),
                pl.BlockSpec((channels, hidden), lambda k: (0, 0)),
            ],
            out_specs=(field_spec,) + (() if last else (pl.BlockSpec(spec_shape, lambda k: (0, 0)),)),
            scratch_shapes=[pltpu.VMEM((lines, chunk) if last else spec_shape, F32)],
            name="layer",
        )(modes, table, field, mlp_up[number], mlp_down[number])
        if last:
            field = results[0]
        else:
            field, spec = results

    picked = pl.pallas_call(
        functools.partial(pick_kernel, cap, per_plane),
        out_shape=jax.ShapeDtypeStruct((devices, cap, channels, size), BF16),
        in_specs=[SMEM, VMEM],
        out_specs=VMEM,
        name="pick",
    )(wanted, field)
    fetched = swap(picked).reshape(devices * cap, channels, size)
    return pl.pallas_call(
        decode_kernel,
        out_shape=jax.ShapeDtypeStruct((channels, pairs // NBR * size), F32),
        in_specs=[SMEM, VMEM, VMEM],
        out_specs=VMEM,
        name="decode",
    )(slot_of, fetched, pair_kernel)


def solution(mesh):
    in_specs = (
        P(None, ("groups", "pen")),
        P(("groups", "pen"), None, None),
        P(("groups", "pen"), None),
        P(("groups", "pen")),
        P(None, "pen", None, None, None),
        P(),
        P(),
    )
    out_specs = P(None, ("groups", "pen"))
    return jax.shard_map(
        per_device, mesh=mesh, in_specs=in_specs, out_specs=out_specs, check_vma=False
    )
```

```python
import functools
import math

import jax
import jax.numpy as jnp
import numpy as np
from jax import lax
from jax.experimental import pallas as pl
from jax.experimental.pallas import tpu as pltpu
from jax.sharding import PartitionSpec as P

NX = 128
NY = 64
NZ = 64
MX = 16
MY = 16
MZ = 16
LAYERS = 2
NBR = 4

F32 = jnp.float32
BF16 = jnp.bfloat16
VMEM = pl.BlockSpec(memory_space=pltpu.VMEM)
SMEM = pl.BlockSpec(memory_space=pltpu.SMEM)
NT = (((1,), (1,)), ((), ()))


def plane_table(devices, lanes):
    here = MY * MZ // devices
    row = np.arange(2 * MY * MZ)
    mode = row // (2 * here) * here + row % here
    imag = (row % (2 * here)) // here
    wave_y = mode // MZ - MY // 2
    wave_z = mode % MZ
    cell = np.arange(lanes)
    turns = np.mod(np.outer(wave_y, cell // NZ), NY) / NY + np.mod(np.outer(wave_z, cell % NZ), NZ) / NZ
    first = 2 * np.pi * turns + np.where(imag, np.pi / 2, 0.0)[:, None]
    tiles = NY * NZ // lanes
    step = 2 * np.pi * np.mod(np.outer(np.arange(tiles) * (lanes // NZ), wave_y), NY) / NY
    parts = [np.cos(first), np.sin(first), np.cos(step), np.sin(step)]
    cos0, sin0, cos_k, sin_k = lax.optimization_barrier(tuple(jnp.asarray(a, F32) for a in parts))
    return (cos0[None] * cos_k[:, :, None] - sin0[None] * sin_k[:, :, None]).astype(BF16)


def along_tables(devices):
    planes = NX // devices
    waves = np.arange(MX) - MX // 2
    angle = 2 * np.pi * np.mod(np.outer(waves, np.arange(NX)), NX) / NX
    cos = np.cos(angle).reshape(MX, devices, planes)
    sin = np.sin(angle).reshape(MX, devices, planes)
    to_real = np.stack([cos, sin], axis=2)
    to_imag = np.stack([-sin, cos], axis=2)
    forward = np.concatenate([to_real, to_imag], axis=0).reshape(2 * MX, 2 * NX)
    high = forward.astype(jnp.bfloat16).astype(np.float64)
    both = np.concatenate([high, forward - high], axis=0)
    return jnp.asarray(both, BF16), jnp.asarray(both.T, BF16)


def encode_kernel(devices, cap, owner, block, feat, kern, send, slot_of, targets, count):
    pairs = kern.shape[0]
    size = kern.shape[1]

    def clear(d, carry):
        count[d] = 0
        for i in range(cap):
            targets[d * cap + i] = -1
        send[d] = jnp.zeros(send.shape[1:], BF16)
        return carry

    lax.fori_loop(0, devices, clear, 0)

    def one(b, carry):
        values = feat[:, pl.ds(pl.multiple_of(b * size, size), size)]
        for k in range(NBR):
            p = b * NBR + k
            d = owner[p]
            n = count[d]
            count[d] = n + 1
            slot_of[p] = d * cap + n
            targets[d * cap + n] = block[p]
            send[d, n] = jnp.dot(values, kern[p], preferred_element_type=F32).astype(BF16)
        return carry

    lax.fori_loop(0, pairs // NBR, one, 0)
    lane = lax.broadcasted_iota(jnp.int32, (16, size), 1)

    def note(d, carry):
        row = jnp.zeros((16, size), F32)
        for i in range(cap):
            row = jnp.where(lane == i, targets[d * cap + i].astype(F32), row)
        send[d, cap, 0:16, :] = row.astype(BF16)
        return carry

    lax.fori_loop(0, devices, note, 0)


def table_tile(table, k, wide):
    return jnp.concatenate([table[k * wide + i] for i in range(wide)], axis=1)


def gather_sums_kernel(cap, per_plane, wide, targets, got, table, field, spec, total):
    channels, size = got.shape[2], got.shape[3]
    chunk = wide * size
    tiles = table.shape[0] // wide

    def clear(k, carry):
        field[:, pl.ds(pl.multiple_of(k * chunk, chunk), chunk)] = jnp.zeros((field.shape[0], chunk), F32)
        return carry

    lax.fori_loop(0, tiles, clear, 0)

    def add(d, carry):
        for i in range(cap):
            t = targets[d * cap + i]

            @pl.when(t >= 0)
            def _():
                rows = pl.ds(pl.multiple_of(t // per_plane * channels, channels), channels)
                cols = pl.ds(pl.multiple_of(t % per_plane * size, size), size)
                field[rows, cols] += got[d, i].astype(F32)

        return carry

    lax.fori_loop(0, got.shape[0], add, 0)
    total[...] = jnp.zeros_like(total)

    def transform(k, carry):
        values = field[:, pl.ds(pl.multiple_of(k * chunk, chunk), chunk)].astype(BF16)
        total[...] += lax.dot_general(table_tile(table, k, wide), values, NT, preferred_element_type=F32)
        return carry

    lax.fori_loop(0, tiles, transform, 0)
    spec[...] = total[...].astype(BF16)


def mix_kernel(channels, forward, inverse, data, weight, scaling, out, mixed):
    rows = 2 * MX
    here, fan = weight.shape[0], weight.shape[1] // (2 * channels)
    width = 2 * channels
    row_wave = lax.broadcasted_iota(jnp.int32, (rows, width), 0) % MX
    half = lax.broadcasted_iota(jnp.int32, (rows, width), 1) // channels
    left = half == 0
    modes = jnp.dot(forward[...], data[...], preferred_element_type=F32)
    modes = modes[:rows] + modes[rows:]
    for pair in range(here // 2):
        own = modes[:, pair * width : (pair + 1) * width]
        other = pltpu.roll(own, channels, 1)
        halves = []
        for k in range(2):
            twice = jnp.where(left, own, other) if k == 0 else jnp.where(left, other, own)
            spread = jnp.concatenate(
                [jnp.where(row_wave == 2 * f + half, twice, 0.0).astype(BF16) for f in range(fan)], axis=1
            )
            prod = jnp.dot(spread, weight[2 * pair + k], preferred_element_type=F32)
            real, imag = prod[:MX], prod[MX:]
            real_turned = pltpu.roll(real, channels, 1)
            imag_turned = pltpu.roll(imag, channels, 1)
            if k == 0:
                halves.append((real - imag_turned, real_turned + imag))
            else:
                halves.append((real_turned - imag, real + imag_turned))
        (real_a, imag_a), (real_b, imag_b) = halves
        top = left[:MX]
        both = jnp.concatenate([jnp.where(top, real_a, real_b), jnp.where(top, imag_a, imag_b)], axis=0)
        both = (both * scaling[:, pair * width : (pair + 1) * width]).astype(BF16)
        mixed[0:rows, pair * width : (pair + 1) * width] = both
        mixed[rows : 2 * rows, pair * width : (pair + 1) * width] = both
    out[...] = jnp.dot(inverse[...], mixed[...], preferred_element_type=F32).astype(BF16)


def layer_kernel(last, planes, wide, modes, table, field, up, down, out, *rest):
    channels = field.shape[0] // planes
    tile = table_tile(table, 0, wide)
    summed = out if not last else rest[0]
    summed[...] = field[...] + jnp.dot(modes[...], tile, preferred_element_type=F32)
    scale = math.sqrt(2.0 / math.pi)
    down_half = (down[...].astype(F32) * 0.5).astype(BF16)

    def raise_up(p):
        values = summed[p * channels : (p + 1) * channels, :]
        return jnp.dot(up[...], values.astype(BF16), preferred_element_type=F32).astype(BF16)

    ahead = raise_up(0)
    for p in range(planes):
        v = ahead
        if p + 1 < planes:
            ahead = raise_up(p + 1)
        rows = slice(p * channels, (p + 1) * channels)
        turn = jnp.tanh(v * (BF16(scale) + BF16(scale * 0.044715) * (v * v)))
        active = v + v * turn
        values = summed[rows, :] + jnp.dot(down_half, active, preferred_element_type=F32)
        out[rows, :] = values.astype(out.dtype)

    if not last:
        spec, total = rest

        @pl.when(pl.program_id(0) == 0)
        def _():
            total[...] = jnp.zeros_like(total)

        total[...] += lax.dot_general(tile, out[...].astype(BF16), NT, preferred_element_type=F32)

        @pl.when(pl.program_id(0) == pl.num_programs(0) - 1)
        def _():
            spec[...] = total[...].astype(BF16)


def pick_kernel(cap, per_plane, targets, field, send):
    channels, size = send.shape[2], send.shape[3]

    def one(d, carry):
        for i in range(cap):
            t = jnp.maximum(targets[d * cap + i], 0)
            rows = pl.ds(pl.multiple_of(t // per_plane * channels, channels), channels)
            cols = pl.ds(pl.multiple_of(t % per_plane * size, size), size)
            send[d, i] = field[rows, cols]
        return carry

    lax.fori_loop(0, send.shape[0], one, 0)


def decode_kernel(slot_of, got, kern, out):
    size = kern.shape[1]

    def one(b, carry):
        acc = None
        for k in range(NBR):
            p = b * NBR + k
            term = lax.dot_general(got[slot_of[p]], kern[p], NT, preferred_element_type=F32)
            acc = term if acc is None else acc + term
        out[:, pl.ds(pl.multiple_of(b * size, size), size)] = acc
        return carry

    lax.fori_loop(0, kern.shape[0] // NBR, one, 0)


def swap(values):
    return lax.all_to_all(values, "pen", split_axis=0, concat_axis=0, tiled=True)


def per_device(point_feat, pair_kernel, pair_owner, pair_block, spec_weight, mlp_up, mlp_down):
    devices = lax.axis_size("pen")
    pairs, size = pair_kernel.shape[0], pair_kernel.shape[1]
    channels = point_feat.shape[0]
    cap = 2 * pairs // devices
    planes = NX // devices
    plane_cells = NY * NZ
    per_plane = plane_cells // size
    here = spec_weight.shape[1]
    modes_all = MY * MZ
    hidden = mlp_up.shape[1]
    lines = planes * channels
    wide = 4
    table = plane_table(devices, size)
    forward, inverse = along_tables(devices)

    send, slot_of, targets = pl.pallas_call(
        functools.partial(encode_kernel, devices, cap),
        out_shape=(
            jax.ShapeDtypeStruct((devices, cap + 1, channels, size), BF16),
            jax.ShapeDtypeStruct((pairs,), jnp.int32),
            jax.ShapeDtypeStruct((devices * cap,), jnp.int32),
        ),
        in_specs=[SMEM, SMEM, VMEM, VMEM],
        out_specs=(VMEM, SMEM, SMEM),
        scratch_shapes=[pltpu.SMEM((devices,), jnp.int32)],
        name="encode",
    )(pair_owner[:, 0], pair_block, point_feat, pair_kernel)
    got = swap(send)
    wanted = got[:, cap, 0, :cap].astype(jnp.int32).reshape(devices * cap)

    field, spec = pl.pallas_call(
        functools.partial(gather_sums_kernel, cap, per_plane, wide),
        out_shape=(
            jax.ShapeDtypeStruct((lines, plane_cells), F32),
            jax.ShapeDtypeStruct((2 * modes_all, lines), BF16),
        ),
        in_specs=[SMEM, VMEM, VMEM],
        out_specs=(VMEM, VMEM),
        scratch_shapes=[pltpu.VMEM((2 * modes_all, lines), F32)],
        name="place",
    )(wanted, got, table)

    first_mode = lax.axis_index("pen") * here
    wave_z = (first_mode + jnp.arange(here * channels, dtype=jnp.int32) // channels) % MZ
    scaling = (jnp.where(wave_z == 0, 1.0, 2.0).astype(F32) / (NX * NY * NZ))[None, :]
    weights = spec_weight.reshape(LAYERS * here, MX * channels, 2 * channels)
    whole = lambda shape: pl.BlockSpec(shape, lambda g: (0,) * len(shape))
    for number in range(LAYERS):
        last = number == LAYERS - 1
        across = swap(spec.reshape(devices, 2 * here, lines))
        data = across.reshape(devices, 2, here, planes, channels).transpose(0, 1, 3, 2, 4)
        mixed = pl.pallas_call(
            functools.partial(mix_kernel, channels),
            out_shape=jax.ShapeDtypeStruct((2 * NX, here * channels), BF16),
            grid=(1,),
            in_specs=[
                whole((4 * MX, 2 * NX)),
                whole((2 * NX, 4 * MX)),
                whole((2 * NX, here * channels)),
                pl.BlockSpec((here, MX * channels, 2 * channels), lambda g, n=number: (n, 0, 0)),
                whole((1, here * channels)),
            ],
            out_specs=whole((2 * NX, here * channels)),
            scratch_shapes=[pltpu.VMEM((4 * MX, here * channels), BF16)],
            name="mix",
        )(forward, inverse, data.reshape(2 * NX, here * channels), weights, scaling)
        modes = swap(mixed.reshape(devices, 2 * planes, here * channels))
        modes = modes.reshape(devices, 2, planes, here, channels).transpose(0, 1, 3, 2, 4)
        modes = modes.reshape(2 * modes_all, lines).T

        chunk = wide * size
        spec_shape = (2 * modes_all, lines)
        field_spec = pl.BlockSpec((lines, chunk), lambda k: (0, k))
        results = pl.pallas_call(
            functools.partial(layer_kernel, last, planes, wide),
            out_shape=(jax.ShapeDtypeStruct((lines, plane_cells), BF16 if last else F32),)
            + (() if last else (jax.ShapeDtypeStruct(spec_shape, BF16),)),
            grid=(plane_cells // chunk,),
            in_specs=[
                pl.BlockSpec((lines, 2 * modes_all), lambda k: (0, 0)),
                pl.BlockSpec((wide, 2 * modes_all, size), lambda k: (k, 0, 0)),
                field_spec,
                pl.BlockSpec((hidden, channels), lambda k: (0, 0)),
                pl.BlockSpec((channels, hidden), lambda k: (0, 0)),
            ],
            out_specs=(field_spec,) + (() if last else (pl.BlockSpec(spec_shape, lambda k: (0, 0)),)),
            scratch_shapes=[pltpu.VMEM((lines, chunk) if last else spec_shape, F32)],
            name="layer",
        )(modes, table, field, mlp_up[number], mlp_down[number])
        if last:
            field = results[0]
        else:
            field, spec = results

    picked = pl.pallas_call(
        functools.partial(pick_kernel, cap, per_plane),
        out_shape=jax.ShapeDtypeStruct((devices, cap, channels, size), BF16),
        in_specs=[SMEM, VMEM],
        out_specs=VMEM,
        name="pick",
    )(wanted, field)
    fetched = swap(picked).reshape(devices * cap, channels, size)
    return pl.pallas_call(
        decode_kernel,
        out_shape=jax.ShapeDtypeStruct((channels, pairs // NBR * size), F32),
        in_specs=[SMEM, VMEM, VMEM],
        out_specs=VMEM,
        name="decode",
    )(slot_of, fetched, pair_kernel)


def solution(mesh):
    in_specs = (
        P(None, ("groups", "pen")),
        P(("groups", "pen"), None, None),
        P(("groups", "pen"), None),
        P(("groups", "pen")),
        P(None, "pen", None, None, None),
        P(),
        P(),
    )
    out_specs = P(None, ("groups", "pen"))
    return jax.shard_map(
        per_device, mesh=mesh, in_specs=in_specs, out_specs=out_specs, check_vma=False
    )
```

```python
import functools
import math

import jax
import jax.numpy as jnp
import numpy as np
from jax import lax
from jax.experimental import pallas as pl
from jax.experimental.pallas import tpu as pltpu
from jax.sharding import PartitionSpec as P

NX = 128
NY = 64
NZ = 64
MX = 16
MY = 16
MZ = 16
LAYERS = 2
NBR = 4
PARTS = 2
NOTE_ROWS = 16

F32 = jnp.float32
BF16 = jnp.bfloat16
VMEM = pl.BlockSpec(memory_space=pltpu.VMEM)
SMEM = pl.BlockSpec(memory_space=pltpu.SMEM)
NT = (((1,), (1,)), ((), ()))


def plane_table(devices, lanes):
    here = MY * MZ // devices
    row = np.arange(2 * MY * MZ)
    mode = row // (2 * here) * here + row % here
    imag = (row % (2 * here)) // here
    wave_y = mode // MZ - MY // 2
    wave_z = mode % MZ
    cell = np.arange(lanes)
    turns = np.mod(np.outer(wave_y, cell // NZ), NY) / NY + np.mod(np.outer(wave_z, cell % NZ), NZ) / NZ
    first = 2 * np.pi * turns + np.where(imag, np.pi / 2, 0.0)[:, None]
    tiles = NY * NZ // lanes
    step = 2 * np.pi * np.mod(np.outer(np.arange(tiles) * (lanes // NZ), wave_y), NY) / NY
    parts = [np.cos(first), np.sin(first), np.cos(step), np.sin(step)]
    cos0, sin0, cos_k, sin_k = lax.optimization_barrier(tuple(jnp.asarray(a, F32) for a in parts))
    return (cos0[None] * cos_k[:, :, None] - sin0[None] * sin_k[:, :, None]).astype(BF16)


def along_tables(devices):
    planes = NX // devices
    waves = np.arange(MX) - MX // 2
    angle = 2 * np.pi * np.mod(np.outer(waves, np.arange(NX)), NX) / NX
    cos = np.cos(angle).reshape(MX, devices, PARTS, planes // PARTS)
    sin = np.sin(angle).reshape(MX, devices, PARTS, planes // PARTS)
    to_real = np.stack([cos, sin], axis=3)
    to_imag = np.stack([-sin, cos], axis=3)
    forward = np.concatenate([to_real, to_imag], axis=0).transpose(2, 0, 1, 3, 4)
    forward = forward.reshape(PARTS, 2 * MX, 2 * NX // PARTS)
    high = forward.astype(jnp.bfloat16).astype(np.float64)
    both = np.concatenate([high, forward - high], axis=1)
    return jnp.asarray(both, BF16), jnp.asarray(both.transpose(0, 2, 1), BF16)


def encode_kernel(devices, cap, owner, block, feat, kern, send, slot_of, targets, count):
    pairs = kern.shape[0]
    size = kern.shape[1]

    def clear(d, carry):
        count[d] = 0
        for i in range(cap):
            targets[d * cap + i] = -1
        send[d] = jnp.zeros(send.shape[1:], BF16)
        return carry

    lax.fori_loop(0, devices, clear, 0)

    def one(b, carry):
        values = feat[:, pl.ds(pl.multiple_of(b * size, size), size)]
        for k in range(NBR):
            p = b * NBR + k
            d = owner[p]
            n = count[d]
            count[d] = n + 1
            slot_of[p] = d * cap + n
            targets[d * cap + n] = block[p]
            rows = pl.ds(pl.multiple_of(n * values.shape[0], values.shape[0]), values.shape[0])
            send[d, rows, :] = jnp.dot(values, kern[p], preferred_element_type=F32).astype(BF16)
        return carry

    lax.fori_loop(0, pairs // NBR, one, 0)
    lane = lax.broadcasted_iota(jnp.int32, (NOTE_ROWS, size), 1)

    def note(d, carry):
        row = jnp.zeros((NOTE_ROWS, size), F32)
        for i in range(cap):
            row = jnp.where(lane == i, targets[d * cap + i].astype(F32), row)
        send[d, send.shape[1] - NOTE_ROWS :, :] = row.astype(BF16)
        return carry

    lax.fori_loop(0, devices, note, 0)


def table_tile(table, k, wide):
    return jnp.concatenate([table[k * wide + i] for i in range(wide)], axis=1)


def gather_sums_kernel(cap, channels, part, per_plane, wide, targets, got, table, field, spec, total):
    size = got.shape[2]
    blocks = field.shape[0] // channels * per_plane
    chunk = wide * size
    tiles = table.shape[0] // wide

    def clear(k, carry):
        field[:, pl.ds(pl.multiple_of(k * chunk, chunk), chunk)] = jnp.zeros((field.shape[0], chunk), F32)
        return carry

    lax.fori_loop(0, tiles, clear, 0)

    def add(d, carry):
        for i in range(cap):
            t = targets[d * cap + i] - part * blocks

            @pl.when((t >= 0) & (t < blocks))
            def _():
                rows = pl.ds(pl.multiple_of(t // per_plane * channels, channels), channels)
                cols = pl.ds(pl.multiple_of(t % per_plane * size, size), size)
                field[rows, cols] += got[d, i * channels : (i + 1) * channels, :].astype(F32)

        return carry

    lax.fori_loop(0, got.shape[0], add, 0)
    total[...] = jnp.zeros_like(total)

    def transform(k, carry):
        values = field[:, pl.ds(pl.multiple_of(k * chunk, chunk), chunk)].astype(BF16)
        total[...] += lax.dot_general(table_tile(table, k, wide), values, NT, preferred_element_type=F32)
        return carry

    lax.fori_loop(0, tiles, transform, 0)
    spec[...] = total[...].astype(BF16)


def mix_kernel(channels, forward, inverse, *refs):
    datas, (weight, scaling), outs, mixed = refs[:PARTS], refs[PARTS : PARTS + 2], refs[PARTS + 2 : -1], refs[-1]
    rows = 2 * MX
    here, fan = weight.shape[0], weight.shape[1] // (2 * channels)
    width = 2 * channels
    row_wave = lax.broadcasted_iota(jnp.int32, (rows, width), 0) % MX
    half = lax.broadcasted_iota(jnp.int32, (rows, width), 1) // channels
    left = half == 0
    modes = sum(jnp.dot(forward[i], datas[i][...], preferred_element_type=F32) for i in range(PARTS))
    modes = modes[:rows] + modes[rows:]
    for pair in range(here // 2):
        own = modes[:, pair * width : (pair + 1) * width]
        other = pltpu.roll(own, channels, 1)
        halves = []
        for k in range(2):
            twice = jnp.where(left, own, other) if k == 0 else jnp.where(left, other, own)
            spread = jnp.concatenate(
                [jnp.where(row_wave == 2 * f + half, twice, 0.0).astype(BF16) for f in range(fan)], axis=1
            )
            prod = jnp.dot(spread, weight[2 * pair + k], preferred_element_type=F32)
            real, imag = prod[:MX], prod[MX:]
            real_turned = pltpu.roll(real, channels, 1)
            imag_turned = pltpu.roll(imag, channels, 1)
            if k == 0:
                halves.append((real - imag_turned, real_turned + imag))
            else:
                halves.append((real_turned - imag, real + imag_turned))
        (real_a, imag_a), (real_b, imag_b) = halves
        top = left[:MX]
        both = jnp.concatenate([jnp.where(top, real_a, real_b), jnp.where(top, imag_a, imag_b)], axis=0)
        both = (both * scaling[:, pair * width : (pair + 1) * width]).astype(BF16)
        mixed[0:rows, pair * width : (pair + 1) * width] = both
        mixed[rows : 2 * rows, pair * width : (pair + 1) * width] = both
    for i in range(PARTS):
        outs[i][...] = jnp.dot(inverse[i], mixed[...], preferred_element_type=F32).astype(BF16)


def layer_kernel(last, planes, wide, modes, table, field, up, down, out, *rest):
    channels = field.shape[0] // planes
    tile = table_tile(table, 0, wide)
    summed = out if not last else rest[0]
    summed[...] = field[...] + jnp.dot(modes[...], tile, preferred_element_type=F32)
    scale = math.sqrt(2.0 / math.pi)
    down_half = (down[...].astype(F32) * 0.5).astype(BF16)

    def raise_up(p):
        values = summed[p * channels : (p + 1) * channels, :]
        return jnp.dot(up[...], values.astype(BF16), preferred_element_type=F32).astype(BF16)

    ahead = raise_up(0)
    for p in range(planes):
        v = ahead
        if p + 1 < planes:
            ahead = raise_up(p + 1)
        rows = slice(p * channels, (p + 1) * channels)
        turn = jnp.tanh(v * (BF16(scale) + BF16(scale * 0.044715) * (v * v)))
        active = v + v * turn
        values = summed[rows, :] + jnp.dot(down_half, active, preferred_element_type=F32)
        out[rows, :] = values.astype(out.dtype)

    if not last:
        spec, total = rest

        @pl.when(pl.program_id(0) == 0)
        def _():
            total[...] = jnp.zeros_like(total)

        total[...] += lax.dot_general(tile, out[...].astype(BF16), NT, preferred_element_type=F32)

        @pl.when(pl.program_id(0) == pl.num_programs(0) - 1)
        def _():
            spec[...] = total[...].astype(BF16)


def pick_kernel(cap, per_plane, targets, *refs):
    fields, send = refs[:-1], refs[-1]
    channels, size = send.shape[2], send.shape[3]
    blocks = fields[0].shape[0] // channels * per_plane

    def one(d, carry):
        for i in range(cap):
            wanted = jnp.maximum(targets[d * cap + i], 0)
            for part, field in enumerate(fields):
                t = wanted - part * blocks

                @pl.when((t >= 0) & (t < blocks))
                def _():
                    rows = pl.ds(pl.multiple_of(t // per_plane * channels, channels), channels)
                    cols = pl.ds(pl.multiple_of(t % per_plane * size, size), size)
                    send[d, i] = field[rows, cols]

        return carry

    lax.fori_loop(0, send.shape[0], one, 0)


def decode_kernel(slot_of, got, kern, out):
    size = kern.shape[1]

    def one(b, carry):
        acc = None
        for k in range(NBR):
            p = b * NBR + k
            term = lax.dot_general(got[slot_of[p]], kern[p], NT, preferred_element_type=F32)
            acc = term if acc is None else acc + term
        out[:, pl.ds(pl.multiple_of(b * size, size), size)] = acc
        return carry

    lax.fori_loop(0, kern.shape[0] // NBR, one, 0)


def cost(flops, moved):
    return pl.CostEstimate(flops=flops, bytes_accessed=moved, transcendentals=0)


def swap(values):
    return lax.all_to_all(values, "pen", split_axis=0, concat_axis=0, tiled=True)


def per_device(point_feat, pair_kernel, pair_owner, pair_block, spec_weight, mlp_up, mlp_down):
    devices = lax.axis_size("pen")
    pairs, size = pair_kernel.shape[0], pair_kernel.shape[1]
    channels = point_feat.shape[0]
    cap = 2 * pairs // devices
    planes = NX // devices
    plane_cells = NY * NZ
    per_plane = plane_cells // size
    here = spec_weight.shape[1]
    modes_all = MY * MZ
    hidden = mlp_up.shape[1]
    lines = planes * channels
    wide = 4
    table = plane_table(devices, size)
    forward, inverse = along_tables(devices)

    send, slot_of, targets = pl.pallas_call(
        functools.partial(encode_kernel, devices, cap),
        out_shape=(
            jax.ShapeDtypeStruct((devices, cap * channels + NOTE_ROWS, size), BF16),
            jax.ShapeDtypeStruct((pairs,), jnp.int32),
            jax.ShapeDtypeStruct((devices * cap,), jnp.int32),
        ),
        in_specs=[SMEM, SMEM, VMEM, VMEM],
        out_specs=(VMEM, SMEM, SMEM),
        scratch_shapes=[pltpu.SMEM((devices,), jnp.int32)],
        name="encode",
    )(pair_owner[:, 0], pair_block, point_feat, pair_kernel)
    got = swap(send)
    wanted = got[:, cap * channels, :cap].astype(jnp.int32).reshape(devices * cap)

    lines = lines // PARTS
    half_planes = planes // PARTS
    fields, specs = [], []
    for part in range(PARTS):
        field, spec = pl.pallas_call(
            functools.partial(gather_sums_kernel, cap, channels, part, per_plane, wide),
            out_shape=(
                jax.ShapeDtypeStruct((lines, plane_cells), F32),
                jax.ShapeDtypeStruct((2 * modes_all, lines), BF16),
            ),
            in_specs=[SMEM, VMEM, VMEM],
            out_specs=(VMEM, VMEM),
            scratch_shapes=[pltpu.VMEM((2 * modes_all, lines), F32)],
            cost_estimate=cost(4 * modes_all * lines * plane_cells, 4 * lines * plane_cells),
            name="place",
        )(wanted, got, table)
        fields.append(field)
        specs.append(spec)

    first_mode = lax.axis_index("pen") * here
    wave_z = (first_mode + jnp.arange(here * channels, dtype=jnp.int32) // channels) % MZ
    scaling = (jnp.where(wave_z == 0, 1.0, 2.0).astype(F32) / (NX * NY * NZ))[None, :]
    weights = spec_weight.reshape(LAYERS * here, MX * channels, 2 * channels)
    whole = lambda shape: pl.BlockSpec(shape, lambda g: (0,) * len(shape))
    for number in range(LAYERS):
        last = number == LAYERS - 1
        datas = []
        for spec in specs:
            across = swap(spec.reshape(devices, 2 * here, lines))
            across = across.reshape(devices, 2, here, half_planes, channels).transpose(0, 1, 3, 2, 4)
            datas.append(across.reshape(2 * NX // PARTS, here * channels))
        mixed_shape = (2 * NX // PARTS, here * channels)
        mixed = pl.pallas_call(
            functools.partial(mix_kernel, channels),
            out_shape=(jax.ShapeDtypeStruct(mixed_shape, BF16),) * PARTS,
            grid=(1,),
            in_specs=[whole(forward.shape), whole(inverse.shape)]
            + [whole(mixed_shape)] * PARTS
            + [
                pl.BlockSpec((here, MX * channels, 2 * channels), lambda g, n=number: (n, 0, 0)),
                whole((1, here * channels)),
            ],
            out_specs=(whole(mixed_shape),) * PARTS,
            scratch_shapes=[pltpu.VMEM((4 * MX, here * channels), BF16)],
            name="mix",
        )(forward, inverse, *datas, weights, scaling)

        chunk = wide * size
        spec_shape = (2 * modes_all, lines)
        field_spec = pl.BlockSpec((lines, chunk), lambda k: (0, k))
        specs = []
        backs = [swap(m.reshape(devices, 2 * half_planes, here * channels)) for m in mixed]
        for part in range(PARTS):
            if part:
                backs[part], fields[part - 1] = lax.optimization_barrier((backs[part], fields[part - 1]))
            modes = backs[part].reshape(devices, 2, half_planes, here, channels).transpose(0, 1, 3, 2, 4)
            modes = modes.reshape(2 * modes_all, lines).T
            results = pl.pallas_call(
                functools.partial(layer_kernel, last, half_planes, wide),
                out_shape=(jax.ShapeDtypeStruct((lines, plane_cells), BF16 if last else F32),)
                + (() if last else (jax.ShapeDtypeStruct(spec_shape, BF16),)),
                grid=(plane_cells // chunk,),
                in_specs=[
                    pl.BlockSpec((lines, 2 * modes_all), lambda k: (0, 0)),
                    pl.BlockSpec((wide, 2 * modes_all, size), lambda k: (k, 0, 0)),
                    field_spec,
                    pl.BlockSpec((hidden, channels), lambda k: (0, 0)),
                    pl.BlockSpec((channels, hidden), lambda k: (0, 0)),
                ],
                out_specs=(field_spec,) + (() if last else (pl.BlockSpec(spec_shape, lambda k: (0, 0)),)),
                scratch_shapes=[pltpu.VMEM((lines, chunk) if last else spec_shape, F32)],
                cost_estimate=cost(8 * modes_all * lines * plane_cells, 8 * lines * plane_cells),
                name="layer",
            )(modes, table, fields[part], mlp_up[number], mlp_down[number])
            fields[part] = results[0]
            if not last:
                specs.append(results[1])

    picked = pl.pallas_call(
        functools.partial(pick_kernel, cap, per_plane),
        out_shape=jax.ShapeDtypeStruct((devices, cap, channels, size), BF16),
        in_specs=[SMEM] + [VMEM] * PARTS,
        out_specs=VMEM,
        name="pick",
    )(wanted, *fields)
    fetched = swap(picked).reshape(devices * cap, channels, size)
    return pl.pallas_call(
        decode_kernel,
        out_shape=jax.ShapeDtypeStruct((channels, pairs // NBR * size), F32),
        in_specs=[SMEM, VMEM, VMEM],
        out_specs=VMEM,
        name="decode",
    )(slot_of, fetched, pair_kernel)


def solution(mesh):
    in_specs = (
        P(None, ("groups", "pen")),
        P(("groups", "pen"), None, None),
        P(("groups", "pen"), None),
        P(("groups", "pen")),
        P(None, "pen", None, None, None),
        P(),
        P(),
    )
    out_specs = P(None, ("groups", "pen"))
    return jax.shard_map(
        per_device, mesh=mesh, in_specs=in_specs, out_specs=out_specs, check_vma=False
    )
```

```python
import functools
import math

import jax
import jax.numpy as jnp
import numpy as np
from jax import lax
from jax.experimental import pallas as pl
from jax.experimental.pallas import tpu as pltpu
from jax.sharding import PartitionSpec as P

NX = 128
NY = 64
NZ = 64
MX = 16
MY = 16
MZ = 16
LAYERS = 2
NBR = 4
NOTE_ROWS = 16

F32 = jnp.float32
BF16 = jnp.bfloat16
VMEM = pl.BlockSpec(memory_space=pltpu.VMEM)
SMEM = pl.BlockSpec(memory_space=pltpu.SMEM)
NT = (((1,), (1,)), ((), ()))


def plane_table(devices, lanes):
    here = MY * MZ // devices
    row = np.arange(2 * MY * MZ)
    mode = row // (2 * here) * here + row % here
    imag = (row % (2 * here)) // here
    wave_y = mode // MZ - MY // 2
    wave_z = mode % MZ
    cell = np.arange(lanes)
    turns = np.mod(np.outer(wave_y, cell // NZ), NY) / NY + np.mod(np.outer(wave_z, cell % NZ), NZ) / NZ
    first = 2 * np.pi * turns + np.where(imag, np.pi / 2, 0.0)[:, None]
    tiles = NY * NZ // lanes
    step = 2 * np.pi * np.mod(np.outer(np.arange(tiles) * (lanes // NZ), wave_y), NY) / NY
    parts = [np.cos(first), np.sin(first), np.cos(step), np.sin(step)]
    cos0, sin0, cos_k, sin_k = lax.optimization_barrier(tuple(jnp.asarray(a, F32) for a in parts))
    return (cos0[None] * cos_k[:, :, None] - sin0[None] * sin_k[:, :, None]).astype(BF16)


def along_tables(devices):
    planes = NX // devices
    waves = np.arange(MX) - MX // 2
    angle = 2 * np.pi * np.mod(np.outer(waves, np.arange(NX)), NX) / NX
    cos = np.cos(angle).reshape(MX, devices, planes)
    sin = np.sin(angle).reshape(MX, devices, planes)
    to_real = np.stack([cos, sin], axis=2)
    to_imag = np.stack([-sin, cos], axis=2)
    forward = np.concatenate([to_real, to_imag], axis=0).reshape(2 * MX, 2 * NX)
    high = forward.astype(jnp.bfloat16).astype(np.float64)
    both = np.concatenate([high, forward - high], axis=0)
    return jnp.asarray(both, BF16), jnp.asarray(both.T, BF16)


def encode_kernel(devices, cap, owner, block, feat, kern, send, slot_of, targets, count):
    pairs = kern.shape[0]
    size = kern.shape[1]

    def clear(d, carry):
        count[d] = 0
        for i in range(cap):
            targets[d * cap + i] = -1
        send[d] = jnp.zeros(send.shape[1:], BF16)
        return carry

    lax.fori_loop(0, devices, clear, 0)

    def one(b, carry):
        values = feat[:, pl.ds(pl.multiple_of(b * size, size), size)]
        for k in range(NBR):
            p = b * NBR + k
            d = owner[p]
            n = count[d]
            count[d] = n + 1
            slot_of[p] = d * cap + n
            targets[d * cap + n] = block[p]
            rows = pl.ds(pl.multiple_of(n * values.shape[0], values.shape[0]), values.shape[0])
            send[d, rows, :] = jnp.dot(values, kern[p], preferred_element_type=F32).astype(BF16)
        return carry

    lax.fori_loop(0, pairs // NBR, one, 0)
    lane = lax.broadcasted_iota(jnp.int32, (NOTE_ROWS, size), 1)

    def note(d, carry):
        row = jnp.zeros((NOTE_ROWS, size), F32)
        for i in range(cap):
            row = jnp.where(lane == i, targets[d * cap + i].astype(F32), row)
        send[d, send.shape[1] - NOTE_ROWS :, :] = row.astype(BF16)
        return carry

    lax.fori_loop(0, devices, note, 0)


def table_tile(table, k, wide):
    return jnp.concatenate([table[k * wide + i] for i in range(wide)], axis=1)


def gather_sums_kernel(cap, channels, per_plane, wide, targets, got, table, field, spec, total):
    size = got.shape[2]
    chunk = wide * size
    tiles = table.shape[0] // wide

    def clear(k, carry):
        field[:, pl.ds(pl.multiple_of(k * chunk, chunk), chunk)] = jnp.zeros((field.shape[0], chunk), F32)
        return carry

    lax.fori_loop(0, tiles, clear, 0)

    def add(d, carry):
        for i in range(cap):
            t = targets[d * cap + i]

            @pl.when(t >= 0)
            def _():
                rows = pl.ds(pl.multiple_of(t // per_plane * channels, channels), channels)
                cols = pl.ds(pl.multiple_of(t % per_plane * size, size), size)
                field[rows, cols] += got[d, i * channels : (i + 1) * channels, :].astype(F32)

        return carry

    lax.fori_loop(0, got.shape[0], add, 0)
    total[...] = jnp.zeros_like(total)

    def transform(k, carry):
        values = field[:, pl.ds(pl.multiple_of(k * chunk, chunk), chunk)].astype(BF16)
        total[...] += lax.dot_general(table_tile(table, k, wide), values, NT, preferred_element_type=F32)
        return carry

    lax.fori_loop(0, tiles, transform, 0)
    spec[...] = total[...].astype(BF16)


def mix_kernel(channels, forward, inverse, data, weight, scaling, out, mixed):
    rows = 2 * MX
    here, fan = weight.shape[0], weight.shape[1] // (2 * channels)
    width = 2 * channels
    row_wave = lax.broadcasted_iota(jnp.int32, (rows, width), 0) % MX
    half = lax.broadcasted_iota(jnp.int32, (rows, width), 1) // channels
    left = half == 0
    modes = jnp.dot(forward[...], data[...], preferred_element_type=F32)
    modes = modes[:rows] + modes[rows:]
    for pair in range(here // 2):
        own = modes[:, pair * width : (pair + 1) * width]
        other = pltpu.roll(own, channels, 1)
        halves = []
        for k in range(2):
            twice = jnp.where(left, own, other) if k == 0 else jnp.where(left, other, own)
            spread = jnp.concatenate(
                [jnp.where(row_wave == 2 * f + half, twice, 0.0).astype(BF16) for f in range(fan)], axis=1
            )
            prod = jnp.dot(spread, weight[2 * pair + k], preferred_element_type=F32)
            real, imag = prod[:MX], prod[MX:]
            real_turned = pltpu.roll(real, channels, 1)
            imag_turned = pltpu.roll(imag, channels, 1)
            if k == 0:
                halves.append((real - imag_turned, real_turned + imag))
            else:
                halves.append((real_turned - imag, real + imag_turned))
        (real_a, imag_a), (real_b, imag_b) = halves
        top = left[:MX]
        both = jnp.concatenate([jnp.where(top, real_a, real_b), jnp.where(top, imag_a, imag_b)], axis=0)
        both = (both * scaling[:, pair * width : (pair + 1) * width]).astype(BF16)
        mixed[0:rows, pair * width : (pair + 1) * width] = both
        mixed[rows : 2 * rows, pair * width : (pair + 1) * width] = both
    out[...] = jnp.dot(inverse[...], mixed[...], preferred_element_type=F32).astype(BF16)


def layer_kernel(last, planes, wide, modes, table, field, up, down, out, *rest):
    channels = field.shape[0] // planes
    tile = table_tile(table, 0, wide)
    summed = out if not last else rest[0]
    summed[...] = field[...] + jnp.dot(modes[...], tile, preferred_element_type=F32)
    scale = math.sqrt(2.0 / math.pi)
    down_half = (down[...].astype(F32) * 0.5).astype(BF16)

    def raise_up(p):
        values = summed[p * channels : (p + 1) * channels, :]
        return jnp.dot(up[...], values.astype(BF16), preferred_element_type=F32).astype(BF16)

    ahead = raise_up(0)
    for p in range(planes):
        v = ahead
        if p + 1 < planes:
            ahead = raise_up(p + 1)
        rows = slice(p * channels, (p + 1) * channels)
        turn = jnp.tanh(v * (BF16(scale) + BF16(scale * 0.044715) * (v * v)))
        active = v + v * turn
        values = summed[rows, :] + jnp.dot(down_half, active, preferred_element_type=F32)
        out[rows, :] = values.astype(out.dtype)

    if not last:
        spec, total = rest

        @pl.when(pl.program_id(0) == 0)
        def _():
            total[...] = jnp.zeros_like(total)

        total[...] += lax.dot_general(tile, out[...].astype(BF16), NT, preferred_element_type=F32)

        @pl.when(pl.program_id(0) == pl.num_programs(0) - 1)
        def _():
            spec[...] = total[...].astype(BF16)


def pick_kernel(cap, per_plane, targets, field, send):
    channels, size = send.shape[2], send.shape[3]

    def one(d, carry):
        for i in range(cap):
            t = jnp.maximum(targets[d * cap + i], 0)
            rows = pl.ds(pl.multiple_of(t // per_plane * channels, channels), channels)
            cols = pl.ds(pl.multiple_of(t % per_plane * size, size), size)
            send[d, i] = field[rows, cols]
        return carry

    lax.fori_loop(0, send.shape[0], one, 0)


def decode_kernel(slot_of, got, kern, out):
    size = kern.shape[1]

    def one(b, carry):
        acc = None
        for k in range(NBR):
            p = b * NBR + k
            term = lax.dot_general(got[slot_of[p]], kern[p], NT, preferred_element_type=F32)
            acc = term if acc is None else acc + term
        out[:, pl.ds(pl.multiple_of(b * size, size), size)] = acc
        return carry

    lax.fori_loop(0, kern.shape[0] // NBR, one, 0)


def swap(values):
    return lax.all_to_all(values, "pen", split_axis=0, concat_axis=0, tiled=True)


def per_device(point_feat, pair_kernel, pair_owner, pair_block, spec_weight, mlp_up, mlp_down):
    devices = lax.axis_size("pen")
    pairs, size = pair_kernel.shape[0], pair_kernel.shape[1]
    channels = point_feat.shape[0]
    cap = 2 * pairs // devices
    planes = NX // devices
    plane_cells = NY * NZ
    per_plane = plane_cells // size
    here = spec_weight.shape[1]
    modes_all = MY * MZ
    hidden = mlp_up.shape[1]
    lines = planes * channels
    wide = 4
    table = plane_table(devices, size)
    forward, inverse = along_tables(devices)

    send, slot_of, targets = pl.pallas_call(
        functools.partial(encode_kernel, devices, cap),
        out_shape=(
            jax.ShapeDtypeStruct((devices, cap * channels + NOTE_ROWS, size), BF16),
            jax.ShapeDtypeStruct((pairs,), jnp.int32),
            jax.ShapeDtypeStruct((devices * cap,), jnp.int32),
        ),
        in_specs=[SMEM, SMEM, VMEM, VMEM],
        out_specs=(VMEM, SMEM, SMEM),
        scratch_shapes=[pltpu.SMEM((devices,), jnp.int32)],
        name="encode",
    )(pair_owner[:, 0], pair_block, point_feat, pair_kernel)
    got = swap(send)
    wanted = got[:, cap * channels, :cap].astype(jnp.int32).reshape(devices * cap)

    field, spec = pl.pallas_call(
        functools.partial(gather_sums_kernel, cap, channels, per_plane, wide),
        out_shape=(
            jax.ShapeDtypeStruct((lines, plane_cells), F32),
            jax.ShapeDtypeStruct((2 * modes_all, lines), BF16),
        ),
        in_specs=[SMEM, VMEM, VMEM],
        out_specs=(VMEM, VMEM),
        scratch_shapes=[pltpu.VMEM((2 * modes_all, lines), F32)],
        name="place",
    )(wanted, got, table)

    first_mode = lax.axis_index("pen") * here
    wave_z = (first_mode + jnp.arange(here * channels, dtype=jnp.int32) // channels) % MZ
    scaling = (jnp.where(wave_z == 0, 1.0, 2.0).astype(F32) / (NX * NY * NZ))[None, :]
    weights = spec_weight.reshape(LAYERS * here, MX * channels, 2 * channels)
    whole = lambda shape: pl.BlockSpec(shape, lambda g: (0,) * len(shape))
    for number in range(LAYERS):
        last = number == LAYERS - 1
        across = swap(spec.reshape(devices, 2 * here, lines))
        data = across.reshape(devices, 2, here, planes, channels).transpose(0, 1, 3, 2, 4)
        mixed = pl.pallas_call(
            functools.partial(mix_kernel, channels),
            out_shape=jax.ShapeDtypeStruct((2 * NX, here * channels), BF16),
            grid=(1,),
            in_specs=[
                whole((4 * MX, 2 * NX)),
                whole((2 * NX, 4 * MX)),
                whole((2 * NX, here * channels)),
                pl.BlockSpec((here, MX * channels, 2 * channels), lambda g, n=number: (n, 0, 0)),
                whole((1, here * channels)),
            ],
            out_specs=whole((2 * NX, here * channels)),
            scratch_shapes=[pltpu.VMEM((4 * MX, here * channels), BF16)],
            name="mix",
        )(forward, inverse, data.reshape(2 * NX, here * channels), weights, scaling)
        modes = swap(mixed.reshape(devices, 2 * planes, here * channels))
        modes = modes.reshape(devices, 2, planes, here, channels).transpose(0, 1, 3, 2, 4)
        modes = modes.reshape(2 * modes_all, lines).T

        chunk = wide * size
        spec_shape = (2 * modes_all, lines)
        field_spec = pl.BlockSpec((lines, chunk), lambda k: (0, k))
        results = pl.pallas_call(
            functools.partial(layer_kernel, last, planes, wide),
            out_shape=(jax.ShapeDtypeStruct((lines, plane_cells), BF16 if last else F32),)
            + (() if last else (jax.ShapeDtypeStruct(spec_shape, BF16),)),
            grid=(plane_cells // chunk,),
            in_specs=[
                pl.BlockSpec((lines, 2 * modes_all), lambda k: (0, 0)),
                pl.BlockSpec((wide, 2 * modes_all, size), lambda k: (k, 0, 0)),
                field_spec,
                pl.BlockSpec((hidden, channels), lambda k: (0, 0)),
                pl.BlockSpec((channels, hidden), lambda k: (0, 0)),
            ],
            out_specs=(field_spec,) + (() if last else (pl.BlockSpec(spec_shape, lambda k: (0, 0)),)),
            scratch_shapes=[pltpu.VMEM((lines, chunk) if last else spec_shape, F32)],
            name="layer",
        )(modes, table, field, mlp_up[number], mlp_down[number])
        if last:
            field = results[0]
        else:
            field, spec = results

    picked = pl.pallas_call(
        functools.partial(pick_kernel, cap, per_plane),
        out_shape=jax.ShapeDtypeStruct((devices, cap, channels, size), BF16),
        in_specs=[SMEM, VMEM],
        out_specs=VMEM,
        name="pick",
    )(wanted, field)
    fetched = swap(picked).reshape(devices * cap, channels, size)
    return pl.pallas_call(
        decode_kernel,
        out_shape=jax.ShapeDtypeStruct((channels, pairs // NBR * size), F32),
        in_specs=[SMEM, VMEM, VMEM],
        out_specs=VMEM,
        name="decode",
    )(slot_of, fetched, pair_kernel)


def solution(mesh):
    in_specs = (
        P(None, ("groups", "pen")),
        P(("groups", "pen"), None, None),
        P(("groups", "pen"), None),
        P(("groups", "pen")),
        P(None, "pen", None, None, None),
        P(),
        P(),
    )
    out_specs = P(None, ("groups", "pen"))
    return jax.shard_map(
        per_device, mesh=mesh, in_specs=in_specs, out_specs=out_specs, check_vma=False
    )
```
